32 devices in a mesh: seq: 8 (over z, y), head: 4 (over x, core).
Axes of the slice: x: 2, y: 2, z: 4, core: 2. Of those that a mesh axis runs over, the one named last changes fastest.
Arguments:
- queries: bfloat16 [4096, 2048], P('seq', 'head'), may hold values from -6 to 6
- keys: bfloat16 [4096, 2048], P('seq', 'head'), may hold values from -6 to 6
- values: bfloat16 [4096, 2048], P('seq', 'head'), may hold values from -6 to 6
- level_weights: int32 [16, 20], P('head'), may hold values from 1 to 8
- out_grad: bfloat16 [4096, 2048], P('seq'), may hold values from -6 to 6
Outputs:
- normed: bfloat16 [4096, 2048], P('seq', 'head')
- proj_grad: float32 [2048, 2048], P('seq', 'head')
The draws below stay inside these ranges and needn't reach their ends.
All inputs are finite; a program needn't handle non-finite values.
Results may differ from the reference program's by a relative error of at most 0.0031.
Values sent between devices are 32-bit elements; how exact they have to be, the bound alone decides.
A program may use at most 64 MiB of HBM per device.

```python
import jax
import jax.numpy as jnp
from jax import lax

D = 2048
HEADS = 16
HEAD_DIM = 128
GROUP = 512
LEVELS = 20
TOKENS = 4096


def place_ends(entries, own_key, least, top_value):
    shape = entries.shape
    spot = [jax.random.randint(jax.random.fold_in(own_key, axis), (), 0, shape[axis]) for axis in range(len(shape))]
    entries = entries.at[tuple(spot)].set(least)
    longest = shape.index(max(shape))
    spot[longest] = (spot[longest] + 1) % shape[longest]
    return entries.at[tuple(spot)].set(top_value)


def spiked(drawn, stream_key, source, target, shards_of, factor):
    def block_of(axis_at):
        return (jnp.arange(drawn.shape[axis_at]) // (drawn.shape[axis_at] // shards_of)).reshape((-1,) + (1,) * (drawn.ndim - 1 - axis_at))

    first = jax.random.permutation(stream_key, shards_of)[block_of(target)]
    other_side = (block_of(target) + shards_of // 2) % shards_of
    return jnp.where((block_of(source) == first) | (block_of(source) == other_side), factor * drawn, drawn)


def levels(rng, extent, shards, least, top_value):
    def one(dim, parts):
        heights = jax.random.uniform(jax.random.fold_in(jax.random.fold_in(rng, 6), dim), (parts,), jnp.float32, least / len(shards), top_value / len(shards))
        return jnp.repeat(jnp.exp(heights), extent[dim] // parts).reshape((-1,) + (1,) * (len(extent) - dim - 1))

    gain = one(*shards[0])
    for cut in shards[1:]:
        gain = gain * one(*cut)
    return gain


def noise(rng, extent, spread, most, pieces=(), kind=jnp.bfloat16):
    values = spread * jax.random.normal(rng, extent, jnp.float32)
    if pieces:
        values = values * levels(rng, extent, pieces, -0.22, 0.18)
    return jnp.clip(values, -most, most).astype(kind)


def heavy_noise(stream_key, extent, deviation, most, pieces, heavy, held_as=jnp.bfloat16):
    entries = deviation * jax.random.normal(stream_key, extent, jnp.float32)
    if pieces:
        entries = entries * levels(stream_key, extent, pieces, -0.22, 0.18)
    return jnp.clip(spiked(entries, jax.random.fold_in(stream_key, 3), *heavy), -most, most).astype(held_as)


def setup_inputs(seed: int = 0) -> dict:
    arg_keys = jax.random.split(jax.random.key(seed), 6)
    return {
        "queries": noise(arg_keys[0], (TOKENS, D), 1.0, 6.0, ((0, 8), (1, 4))),
        "keys": noise(arg_keys[1], (TOKENS, D), 1.0, 6.0, ((0, 8), (1, 4))),
        "values": noise(arg_keys[2], (TOKENS, D), 1.0, 6.0, ((0, 8), (1, 4))),
        "level_weights": place_ends(jax.random.randint(arg_keys[3], (HEADS, LEVELS), 1, 9), jax.random.fold_in(arg_keys[3], 1), 1, 8).astype(jnp.int32),
        "out_grad": heavy_noise(arg_keys[4], (TOKENS, D), 1.0, 6.0, ((0, 8),), (0, 1, 8, 2.0)),
    }


def level_table(count):
    index = jnp.arange(count, dtype=jnp.int32)
    mixed = jnp.bitwise_xor(index[:, None], index[None, :])
    level = jnp.zeros((count, count), jnp.int32)
    for bit in range(LEVELS):
        level = level + (mixed >= 2 ** bit).astype(jnp.int32)
    return (level, index)

def one_head(inputs):
    head_q, head_k, head_v, head_w = inputs
    nchunks = TOKENS // GROUP
    scale = HEAD_DIM ** (-0.5)
    qc = head_q.reshape(nchunks, GROUP, HEAD_DIM).astype(jnp.float32)
    kc = head_k.reshape(nchunks, GROUP, HEAD_DIM).astype(jnp.float32)
    vc = head_v.reshape(nchunks, GROUP, HEAD_DIM)
    vf = vc.astype(jnp.float32)
    weights = head_w.astype(jnp.float32)
    state = jnp.einsum('cnd,cne->cde', kc, vf, precision=lax.Precision.HIGHEST)
    level, index = level_table(nchunks)
    table = jnp.where(index[None, :] < index[:, None], jnp.take(weights, level), 0.0)
    mix = jnp.einsum('cj,jde->cde', table, state, precision=lax.Precision.HIGHEST)
    far = scale * jnp.einsum('cnd,cde->cne', qc, mix, precision=lax.Precision.HIGHEST)
    scores = jnp.einsum('cnd,cmd->cnm', qc, kc, precision=lax.Precision.HIGHEST) * (scale * weights[0])
    rows = jnp.arange(GROUP, dtype=jnp.int32)
    causal = rows[None, :] <= rows[:, None]
    probs = jnp.where(causal[None], scores, 0.0).astype(jnp.bfloat16)
    near = jnp.einsum('cnm,cme->cne', probs.astype(jnp.float32), vf, precision=lax.Precision.HIGHEST)
    return (near + far).reshape(TOKENS, HEAD_DIM)

def reference(queries, keys, values, level_weights, out_grad):

    def split(array):
        return array.reshape(TOKENS, HEADS, HEAD_DIM).transpose(1, 0, 2)
    raw = lax.map(one_head, (split(queries), split(keys), split(values), level_weights))
    raw = raw.transpose(1, 0, 2).reshape(TOKENS, D)
    mean_sq = lax.optimization_barrier(jnp.sum(raw * raw, axis=1)) / D
    normed = (raw * lax.rsqrt(mean_sq + 1e-06)[:, None]).astype(jnp.bfloat16)
    proj_grad = jnp.dot(out_grad.T, normed, preferred_element_type=jnp.float32)
    return (normed, proj_grad)
```

```python
import functools

import jax
import jax.numpy as jnp
from jax import lax
from jax.experimental import pallas as pl
from jax.experimental.pallas import tpu as pltpu
from jax.sharding import PartitionSpec as P

D = 2048
HEADS = 16
GROUP = 512
LEVELS = 20
MESH = pl.DeviceIdType.MESH


def partner_2(block, axis, bit):
    count = lax.axis_size(axis)
    route = []
    for low in range(count):
        high = low | 1 << bit
        if high != low and high < count:
            route += [(low, high), (high, low)]
    return lax.ppermute(block, axis, route)


def count_levels(mixed):
    level = jnp.zeros(mixed.shape, jnp.int32)
    for bit in range(LEVELS):
        level = level + (mixed >= 2**bit).astype(jnp.int32)
    return level


def reduce_kernel(
    line,
    chunks,
    lanes,
    grad_ref,
    theirs_ref,
    normed_ref,
    out_ref,
    sent,
    came,
    part,
    rising,
    falling,
    pair_send,
    pair_recv,
    up_send,
    up_recv,
    down_send,
    down_recv,
):
    me = lax.axis_index("seq")
    place = me // 2
    side = me % 2
    other = place * 2 + 1 - side
    above = me + 2
    below = me - 2
    low_end = place == 0
    high_end = place == line - 1
    inner = jnp.logical_and(place > 0, place < line - 1)

    barrier = pltpu.get_barrier_semaphore()
    pl.semaphore_signal(barrier, inc=1, device_id={"seq": other}, device_id_type=MESH)

    @pl.when(place < line - 1)
    def _():
        pl.semaphore_signal(barrier, inc=1, device_id={"seq": above}, device_id_type=MESH)

    @pl.when(place > 0)
    def _():
        pl.semaphore_signal(barrier, inc=1, device_id={"seq": below}, device_id_type=MESH)

    for k in range(chunks):
        sent[k] = normed_ref[:, k * lanes : (k + 1) * lanes].astype(jnp.float32)

    peers = 1 + jnp.where(place > 0, 1, 0) + jnp.where(place < line - 1, 1, 0)
    pl.semaphore_wait(barrier, peers)

    def pair_copy(k):
        return pltpu.make_async_remote_copy(
            src_ref=sent.at[k],
            dst_ref=came.at[k],
            send_sem=pair_send.at[k],
            recv_sem=pair_recv.at[k],
            device_id={"seq": other},
            device_id_type=MESH,
        )

    def up_copy(k, d):
        return pltpu.make_async_remote_copy(
            src_ref=part.at[k, d],
            dst_ref=rising.at[k, d],
            send_sem=up_send.at[k, d],
            recv_sem=up_recv.at[k, d],
            device_id={"seq": above},
            device_id_type=MESH,
        )

    def down_copy(k, d):
        return pltpu.make_async_remote_copy(
            src_ref=part.at[k, d],
            dst_ref=falling.at[k, d],
            send_sem=down_send.at[k, d],
            recv_sem=down_recv.at[k, d],
            device_id={"seq": below},
            device_id_type=MESH,
        )

    for k in range(chunks):
        pair_copy(k).start()

    def ends(k):
        @pl.when(low_end)
        def _():
            @pl.loop(0, line - 1)
            def _(i):
                up_copy(k, line - 1 - i).start()

        @pl.when(high_end)
        def _():
            @pl.loop(0, line - 1)
            def _(d):
                down_copy(k, d).start()

    def middle(k):
        @pl.when(inner)
        def _():
            @pl.loop(0, line - 1 - place)
            def _(i):
                d = line - 1 - i
                up_copy(k, d).wait_recv()
                part[k, d] = part[k, d] + rising[k, d]
                up_copy(k, d).start()

            @pl.loop(0, place)
            def _(d):
                down_copy(k, d).wait_recv()
                part[k, d] = part[k, d] + falling[k, d]
                down_copy(k, d).start()

    theirs = theirs_ref[...].astype(jnp.bfloat16)
    for k in range(chunks):
        pair_copy(k).wait_recv()
        here = normed_ref[:, k * lanes : (k + 1) * lanes]
        there = came[k].astype(jnp.bfloat16)
        total = jnp.dot(grad_ref[...], here, preferred_element_type=jnp.float32)
        total = total + jnp.dot(theirs, there, preferred_element_type=jnp.float32)
        part[k] = total.reshape(part.shape[1:])
        ends(k)
        if k:
            middle(k - 1)
    middle(chunks - 1)

    for k in range(chunks):
        span = slice(k * lanes, (k + 1) * lanes)
        out_ref[:, span] = part[k, place]

        @pl.when(place > 0)
        def _():
            up_copy(k, place).wait_recv()
            out_ref[:, span] = out_ref[:, span] + rising[k, place]

        @pl.when(place < line - 1)
        def _():
            down_copy(k, place).wait_recv()
            out_ref[:, span] = out_ref[:, span] + falling[k, place]

    for k in range(chunks):
        pair_copy(k).wait_send()

        @pl.loop(place + 1, line)
        def _(d):
            up_copy(k, d).wait_send()

        @pl.loop(0, place)
        def _(d):
            down_copy(k, d).wait_send()


def weight_grad(grads, theirs, normed):
    tokens, width = normed.shape
    line = lax.axis_size("seq") // 2
    lanes = D // HEADS
    chunks = width // lanes
    rows = grads.shape[0] // line
    slots = (chunks, line, rows, lanes)
    vmem = pl.BlockSpec(memory_space=pltpu.VMEM)
    return pl.pallas_call(
        functools.partial(reduce_kernel, line, chunks, lanes),
        out_shape=jax.ShapeDtypeStruct((rows, width), jnp.float32),
        in_specs=[vmem, vmem, vmem],
        out_specs=vmem,
        scratch_shapes=[
            pltpu.VMEM((chunks, tokens, lanes), jnp.float32),
            pltpu.VMEM((chunks, tokens, lanes), jnp.float32),
            pltpu.VMEM(slots, jnp.float32),
            pltpu.VMEM(slots, jnp.float32),
            pltpu.VMEM(slots, jnp.float32),
            pltpu.SemaphoreType.DMA((chunks,)),
            pltpu.SemaphoreType.DMA((chunks,)),
            pltpu.SemaphoreType.DMA((chunks, line)),
            pltpu.SemaphoreType.DMA((chunks, line)),
            pltpu.SemaphoreType.DMA((chunks, line)),
            pltpu.SemaphoreType.DMA((chunks, line)),
        ],
        compiler_params=pltpu.CompilerParams(
            collective_id=0, has_side_effects=True, vmem_limit_bytes=40 << 20
        ),
    )(grads, theirs, normed)


def exchange_grads(out_grad):
    tokens = out_grad.shape[0]
    count = lax.axis_size("seq")
    heads = lax.axis_size("head")
    line = count // 2
    side = lax.axis_index("seq") % 2
    head = lax.axis_index("head")
    by_side = lax.optimization_barrier(out_grad.T).reshape(line, 2, D // count, tokens)
    mine = lax.dynamic_index_in_dim(by_side, side, 1, keepdims=False).reshape(D // 2, tokens)
    theirs = lax.dynamic_index_in_dim(by_side, 1 - side, 1, keepdims=False).reshape(D // 2, tokens)
    piece = tokens // heads
    block = lax.dynamic_slice_in_dim(theirs, head * piece, piece, 1).astype(jnp.float32)
    blocks = [partner_2(block, "seq", 0)]
    owners = [head]
    for bit in reversed(range(heads.bit_length() - 1)):
        blocks += [partner_2(block, "head", bit) for block in blocks]
        owners += [jnp.bitwise_xor(owner, 1 << bit) for owner in owners]
    gathered = jnp.zeros((D // 2, tokens), jnp.float32)
    for block, owner in zip(blocks, owners):
        gathered = lax.dynamic_update_slice_in_dim(gathered, block, owner * piece, 1)
    return mine, gathered


def body(queries, keys, values, level_weights, out_grad):
    tok_rows, width = queries.shape
    head_dim = D // HEADS
    heads_here = width // head_dim
    per_dev = tok_rows // GROUP
    local_bits = per_dev.bit_length() - 1
    scale = head_dim ** (-0.5)
    q_blocks = queries.reshape(per_dev, GROUP, heads_here, head_dim)
    k_blocks = keys.reshape(per_dev, GROUP, heads_here, head_dim)
    v_blocks = values.reshape(per_dev, GROUP, heads_here, head_dim)
    weights = level_weights.astype(jnp.float32)
    level_ids = jnp.arange(LEVELS, dtype=jnp.int32)
    state = jnp.einsum("cnhd,cnhe->chde", k_blocks, v_blocks, preferred_element_type=jnp.float32)
    own_state = jnp.sum(state, axis=0)
    local_index = jnp.arange(per_dev, dtype=jnp.int32)
    local_level = count_levels(jnp.bitwise_xor(local_index[:, None], local_index[None, :]))
    earlier = (local_index[None, :] < local_index[:, None]).astype(jnp.float32)
    picker = (local_level[:, :, None] == level_ids[None, None, :]).astype(jnp.float32) * earlier[
        :, :, None
    ]
    local_table = jnp.einsum("cjl,hl->hcj", picker, weights, precision=lax.Precision.HIGHEST)
    mix = jnp.einsum("hcj,jhde->chde", local_table, state, precision=lax.Precision.HIGHEST)
    position = lax.axis_index("seq")
    nbits = lax.axis_size("seq").bit_length() - 1
    grads, theirs = exchange_grads(out_grad)
    block = own_state
    remote = jnp.zeros_like(own_state)
    for bit in range(nbits):
        partner = partner_2(block, "seq", bit)
        upper = jnp.right_shift(position, bit) % 2
        level_weight = weights[:, local_bits + 1 + bit] * upper.astype(jnp.float32)
        remote = remote + level_weight[:, None, None] * partner
        block = block + partner
    mix = mix + remote[None]
    far = scale * jnp.einsum(
        "cnhd,chde->cnhe", q_blocks.astype(jnp.float32), mix, precision=lax.Precision.HIGHEST
    )
    scores = jnp.einsum("cnhd,cmhd->chnm", q_blocks, k_blocks, preferred_element_type=jnp.float32)
    scores = scores * (scale * weights[:, 0])[None, :, None, None]
    rows = jnp.arange(GROUP, dtype=jnp.int32)
    causal = rows[None, :] <= rows[:, None]
    probs = jnp.where(causal[None, None], scores, 0.0).astype(jnp.bfloat16)
    near = jnp.einsum("chnm,cmhe->cnhe", probs, v_blocks, preferred_element_type=jnp.float32)
    raw = (near + far).reshape(tok_rows, width)
    row_squares = lax.psum(jnp.sum(raw * raw, axis=1), "head")
    normed = (raw * lax.rsqrt(row_squares / D + 1e-06)[:, None]).astype(jnp.bfloat16)
    proj_grad = weight_grad(grads, theirs, normed)
    return (normed, proj_grad)


def solution(mesh):
    return jax.shard_map(
        body,
        mesh=mesh,
        in_specs=(
            P("seq", "head"),
            P("seq", "head"),
            P("seq", "head"),
            P("head", None),
            P("seq", None),
        ),
        out_specs=(P("seq", "head"), P("seq", "head")),
        check_vma=False,
    )
```

```python
import functools

import jax
import jax.numpy as jnp
from jax import lax
from jax.experimental import pallas as pl
from jax.experimental.pallas import tpu as pltpu
from jax.sharding import PartitionSpec as P

D = 2048
HEADS = 16
GROUP = 512
MESH = pl.DeviceIdType.MESH
NT = (((1,), (1,)), ((), ()))
TN = (((0,), (0,)), ((), ()))


def flip(index, mask):
    bit = 1
    while bit <= mask:
        if mask & bit:
            index = index + bit - 2 * bit * ((index // bit) % 2)
        bit *= 2
    return index


def matmul(a, b, dims=(((1,), (0,)), ((), ()))):
    return lax.dot_general(a, b, dims, preferred_element_type=jnp.float32)


def split(x):
    high = x.astype(jnp.bfloat16)
    return high, (x - high.astype(jnp.float32)).astype(jnp.bfloat16)


def kernel(
    line,
    heads,
    q_ref,
    k_ref,
    v_ref,
    level_ref,
    grad_ref,
    normed_ref,
    out_ref,
    state,
    pair_state,
    block,
    line_state,
    give,
    mix,
    turned,
    quarter,
    theirs,
    theirs_half,
    raw,
    came,
    squares,
    squares_in,
    root,
    root_in,
    part,
    rising,
    falling,
    state_send,
    state_recv,
    grad_send,
    grad_recv,
    square_send,
    square_recv,
    root_send,
    root_recv,
    pair_send,
    pair_recv,
    up_send,
    up_recv,
    down_send,
    down_recv,
):
    me = lax.axis_index("seq")
    head = lax.axis_index("head")
    place = me // 2
    side = me % 2
    other = flip(me, 1)
    above = me + 2
    below = me - 2
    tokens, width = q_ref.shape
    lanes = D // HEADS
    chunks = width // lanes
    half = chunks // 2
    rows = out_ref.shape[0]
    line_bits = line.bit_length() - 1
    head_bits = heads.bit_length() - 1
    share = line // heads
    scale = lanes ** (-0.5)
    low_end = place == 0
    high_end = place == line - 1
    inner = jnp.logical_and(place > 0, place < line - 1)

    def span(k):
        return slice(k * lanes, (k + 1) * lanes)

    barrier = pltpu.get_barrier_semaphore()

    def greet(device):
        pl.semaphore_signal(barrier, inc=1, device_id=device, device_id_type=MESH)

    greet({"seq": other})
    for b in range(line_bits):
        greet({"seq": flip(me, 2 << b)})
    for r in range(1, heads):
        greet({"head": flip(head, r)})

    @pl.when(place < line - 1)
    def _():
        greet({"seq": above})

    @pl.when(place > 0)
    def _():
        greet({"seq": below})

    def remote(src, dst, send, recv, device):
        return pltpu.make_async_remote_copy(
            src_ref=src,
            dst_ref=dst,
            send_sem=send,
            recv_sem=recv,
            device_id=device,
            device_id_type=MESH,
        )

    def state_copy():
        return remote(
            state.at[pl.ds((1 - side) * half, half)],
            pair_state,
            state_send.at[0],
            state_recv.at[0],
            {"seq": other},
        )

    def line_copy(b):
        return remote(
            block.at[b],
            line_state.at[b],
            state_send.at[1 + b],
            state_recv.at[1 + b],
            {"seq": flip(me, 2 << b)},
        )

    def give_copy():
        return remote(
            give,
            mix.at[pl.ds(side * half, half)],
            state_send.at[1 + line_bits],
            state_recv.at[1 + line_bits],
            {"seq": other},
        )

    def grad_copy():
        return remote(
            quarter,
            theirs.at[pl.ds(head * share, share)],
            grad_send.at[0],
            grad_recv.at[0],
            {"seq": other},
        )

    def share_copy(r, bit):
        owned = theirs.at[pl.ds(flip(head, r) * share, share)]
        slot = r ^ (1 << bit)
        return remote(
            owned, owned, grad_send.at[slot], grad_recv.at[slot], {"head": flip(head, 1 << bit)}
        )

    def square_copy(r):
        return remote(
            squares,
            squares_in.at[r - 1],
            square_send.at[r - 1],
            square_recv.at[r - 1],
            {"head": flip(head, r)},
        )

    def root_copy():
        return remote(root, root_in, root_send.at[0], root_recv.at[0], {"seq": other})

    def pair_copy(k):
        return remote(raw.at[k], came.at[k], pair_send.at[k], pair_recv.at[k], {"seq": other})

    def up_copy(k, d):
        return remote(
            part.at[k, d], rising.at[k, d], up_send.at[k, d], up_recv.at[k, d], {"seq": above}
        )

    def down_copy(k, d):
        return remote(
            part.at[k, d], falling.at[k, d], down_send.at[k, d], down_recv.at[k, d], {"seq": below}
        )

    for h in range(chunks):
        state[h] = matmul(k_ref[:, span(h)], v_ref[:, span(h)], TN)
    peers = line_bits + heads + jnp.where(place > 0, 1, 0) + jnp.where(place < line - 1, 1, 0)
    pl.semaphore_wait(barrier, peers)
    state_copy().start()

    tile = max(rows, lanes)
    for j in range(grad_ref.shape[1] // tile):
        flat = grad_ref[:, j * tile : (j + 1) * tile].T
        for i in range(tile // rows):
            owner = j * (tile // rows) + i
            turned[owner % 2, owner // 2] = flat[i * rows : (i + 1) * rows]
    quarter[...] = turned[1 - side, pl.ds(head * share, share)].astype(jnp.float32)
    grad_copy().start()

    def near(h):
        weight = scale * level_ref[h, 0].astype(jnp.float32)
        scores = matmul(q_ref[:, span(h)], k_ref[:, span(h)], NT) * weight
        row = lax.broadcasted_iota(jnp.int32, scores.shape, 0)
        column = lax.broadcasted_iota(jnp.int32, scores.shape, 1)
        probs = jnp.where(column <= row, scores, 0.0).astype(jnp.bfloat16)
        raw[h] = matmul(probs, v_ref[:, span(h)])

    def level(i, number):
        return level_ref[side * half + i, number].astype(jnp.float32)

    own = pl.ds(side * half, half)
    state_copy().wait_recv()
    block[0] = state[own] + pair_state[...]
    done = 0
    for b in range(line_bits):
        upper = (place // (1 << b)) % 2
        last = b == line_bits - 1
        if last:

            @pl.when(upper == 0)
            def _():
                line_copy(b).start()
        else:
            line_copy(b).start()
        until = chunks * (b + 1) // line_bits
        for h in range(done, until):
            near(h)
        done = until
        if last:

            @pl.when(upper == 1)
            def _():
                line_copy(b).wait_recv()

            @pl.when(upper == 0)
            def _():
                line_state[b] = jnp.zeros(line_state.shape[1:], jnp.float32)
        else:
            line_copy(b).wait_recv()
            block[b + 1] = block[b] + line_state[b]
    for i in range(half):
        far = jnp.zeros((lanes, lanes), jnp.float32)
        for b in range(line_bits):
            upper = ((place // (1 << b)) % 2).astype(jnp.float32)
            far = far + (level(i, 2 + b) * upper) * line_state[b, i]
        first = level(i, 1)
        right = side.astype(jnp.float32)
        mix[side * half + i] = far + (first * right) * pair_state[i]
        give[i] = far + (first * (1.0 - right)) * state[side * half + i]
    give_copy().start()

    owned = [0]
    stages = list(reversed(range(head_bits)))
    grad_copy().wait_recv()

    def forward(bit):
        for r in owned:
            share_copy(r, bit).start()

    def collect(bit):
        for r in list(owned):
            share_copy(r, bit).wait_recv()
            owned.append(r ^ (1 << bit))

    forward(stages[0])
    give_copy().wait_recv()

    total = jnp.zeros((tokens, lanes), jnp.float32)
    for h in range(chunks):
        high, low = split(mix[h])
        query = q_ref[:, span(h)]
        value = raw[h] + scale * (matmul(query, high) + matmul(query, low))
        raw[h] = value
        pair_copy(h).start()
        total = total + value * value
    ones = jnp.ones((8, lanes), jnp.bfloat16)
    high, low = split(total)
    squares[...] = matmul(ones, high, NT) + matmul(ones, low, NT)
    for r in range(1, heads):
        square_copy(r).start()
    collect(stages[0])
    for r in range(1, heads):
        square_copy(r).wait_recv()
    whole = squares[...]
    for r in range(1, heads):
        whole = whole + squares_in[r - 1]
    root[...] = lax.rsqrt(whole / D + 1e-06)
    root_copy().start()
    for bit in stages[1:]:
        forward(bit)
        if bit != stages[-1]:
            collect(bit)
    inverse = root[...].T[:, :1]
    for h in range(chunks):
        normed_ref[:, span(h)] = (raw[h] * inverse).astype(jnp.bfloat16)
    root_copy().wait_recv()
    their_inverse = root_in[...].T[:, :1]
    if len(stages) > 1:
        collect(stages[-1])
    theirs_half[...] = theirs[...].reshape(theirs_half.shape).astype(jnp.bfloat16)

    def ends(k):
        @pl.when(low_end)
        def _():
            @pl.loop(0, line - 1)
            def _(i):
                up_copy(k, line - 1 - i).start()

        @pl.when(high_end)
        def _():
            @pl.loop(0, line - 1)
            def _(d):
                down_copy(k, d).start()

    def middle(k):
        @pl.when(inner)
        def _():
            @pl.loop(0, line - 1 - place)
            def _(i):
                d = line - 1 - i
                up_copy(k, d).wait_recv()
                part[k, d] = part[k, d] + rising[k, d]
                up_copy(k, d).start()

            @pl.loop(0, place)
            def _(d):
                down_copy(k, d).wait_recv()
                part[k, d] = part[k, d] + falling[k, d]
                down_copy(k, d).start()

    for k in range(chunks):
        mine = turned[side].reshape(line * rows, tokens)
        product = matmul(mine, normed_ref[:, span(k)])
        pair_copy(k).wait_recv()
        there = (came[k] * their_inverse).astype(jnp.bfloat16)
        product = product + matmul(theirs_half[...], there)
        part[k] = product.reshape(part.shape[1:])
        ends(k)
        if k:
            middle(k - 1)
    middle(chunks - 1)

    for k in range(chunks):
        out_ref[:, span(k)] = part[k, place]

        @pl.when(place > 0)
        def _():
            up_copy(k, place).wait_recv()
            out_ref[:, span(k)] = out_ref[:, span(k)] + rising[k, place]

        @pl.when(place < line - 1)
        def _():
            down_copy(k, place).wait_recv()
            out_ref[:, span(k)] = out_ref[:, span(k)] + falling[k, place]

    state_copy().wait_send()
    for b in range(line_bits - 1):
        line_copy(b).wait_send()

    @pl.when((place // (line // 2)) % 2 == 0)
    def _():
        line_copy(line_bits - 1).wait_send()

    give_copy().wait_send()
    grad_copy().wait_send()
    held = [0]
    for bit in stages:
        for r in list(held):
            share_copy(r, bit).wait_send()
            held.append(r ^ (1 << bit))
    for r in range(1, heads):
        square_copy(r).wait_send()
    root_copy().wait_send()
    for k in range(chunks):
        pair_copy(k).wait_send()

        @pl.loop(place + 1, line)
        def _(d):
            up_copy(k, d).wait_send()

        @pl.loop(0, place)
        def _(d):
            down_copy(k, d).wait_send()


def body(queries, keys, values, level_weights, out_grad):
    tokens, width = queries.shape
    assert tokens == GROUP
    count = lax.axis_size("seq")
    heads = lax.axis_size("head")
    line = count // 2
    line_bits = line.bit_length() - 1
    lanes = D // HEADS
    chunks = width // lanes
    half = chunks // 2
    rows = out_grad.shape[1] // count
    slots = (chunks, line, rows, lanes)
    states = (half, lanes, lanes)
    vmem = pl.BlockSpec(memory_space=pltpu.VMEM)
    smem = pl.BlockSpec(memory_space=pltpu.SMEM)
    f32 = jnp.float32
    dma = pltpu.SemaphoreType.DMA
    return pl.pallas_call(
        functools.partial(kernel, line, heads),
        out_shape=(
            jax.ShapeDtypeStruct((tokens, width), jnp.bfloat16),
            jax.ShapeDtypeStruct((rows, width), f32),
        ),
        in_specs=[vmem, vmem, vmem, smem, vmem],
        out_specs=(vmem, vmem),
        scratch_shapes=[
            pltpu.VMEM((chunks, lanes, lanes), f32),
            pltpu.VMEM(states, f32),
            pltpu.VMEM((line_bits, *states), f32),
            pltpu.VMEM((line_bits, *states), f32),
            pltpu.VMEM(states, f32),
            pltpu.VMEM((chunks, lanes, lanes), f32),
            pltpu.VMEM((2, line, rows, tokens), jnp.bfloat16),
            pltpu.VMEM((line // heads, rows, tokens), f32),
            pltpu.VMEM((line, rows, tokens), f32),
            pltpu.VMEM((line * rows, tokens), jnp.bfloat16),
            pltpu.VMEM((chunks, tokens, lanes), f32),
            pltpu.VMEM((chunks, tokens, lanes), f32),
            pltpu.VMEM((8, tokens), f32),
            pltpu.VMEM((heads - 1, 8, tokens), f32),
            pltpu.VMEM((8, tokens), f32),
            pltpu.VMEM((8, tokens), f32),
            pltpu.VMEM(slots, f32),
            pltpu.VMEM(slots, f32),
            pltpu.VMEM(slots, f32),
            dma((2 + line_bits,)),
            dma((2 + line_bits,)),
            dma((heads,)),
            dma((heads,)),
            dma((heads - 1,)),
            dma((heads - 1,)),
            dma((1,)),
            dma((1,)),
            dma((chunks,)),
            dma((chunks,)),
            dma((chunks, line)),
            dma((chunks, line)),
            dma((chunks, line)),
            dma((chunks, line)),
        ],
        compiler_params=pltpu.CompilerParams(
            collective_id=0, has_side_effects=True, vmem_limit_bytes=48 << 20
        ),
    )(queries, keys, values, level_weights, out_grad)


def solution(mesh):
    return jax.shard_map(
        body,
        mesh=mesh,
        in_specs=(
            P("seq", "head"),
            P("seq", "head"),
            P("seq", "head"),
            P("head", None),
            P("seq", None),
        ),
        out_specs=(P("seq", "head"), P("seq", "head")),
        check_vma=False,
    )
```

```python
import functools

import jax
import jax.numpy as jnp
from jax import lax
from jax.experimental import pallas as pl
from jax.experimental.pallas import tpu as pltpu
from jax.sharding import PartitionSpec as P

D = 2048
HEADS = 16
GROUP = 512
MESH = pl.DeviceIdType.MESH
NT = (((1,), (1,)), ((), ()))
TN = (((0,), (0,)), ((), ()))


def flip(index, mask):
    bit = 1
    while bit <= mask:
        if mask & bit:
            index = index + bit - 2 * bit * ((index // bit) % 2)
        bit *= 2
    return index


def matmul(a, b, dims=(((1,), (0,)), ((), ()))):
    return lax.dot_general(a, b, dims, preferred_element_type=jnp.float32)


def split(x):
    high = x.astype(jnp.bfloat16)
    return high, (x - high.astype(jnp.float32)).astype(jnp.bfloat16)


def kernel(
    line,
    heads,
    q_in,
    k_in,
    v_in,
    level_ref,
    grad_in,
    normed_ref,
    out_ref,
    q_ref,
    k_ref,
    v_ref,
    grad_ref,
    loads,
    state,
    pair_state,
    block,
    line_state,
    give,
    mix,
    turned,
    quarter,
    theirs,
    theirs_half,
    raw,
    came,
    squares,
    squares_in,
    root,
    root_in,
    part,
    rising,
    falling,
    state_send,
    state_recv,
    grad_send,
    grad_recv,
    square_send,
    square_recv,
    root_send,
    root_recv,
    pair_send,
    pair_recv,
    up_send,
    up_recv,
    down_send,
    down_recv,
):
    me = lax.axis_index("seq")
    head = lax.axis_index("head")
    place = me // 2
    side = me % 2
    other = flip(me, 1)
    above = me + 2
    below = me - 2
    tokens, width = q_ref.shape
    lanes = D // HEADS
    chunks = width // lanes
    half = chunks // 2
    rows = out_ref.shape[0]
    line_bits = line.bit_length() - 1
    head_bits = heads.bit_length() - 1
    share = line // heads
    scale = lanes ** (-0.5)
    low_end = place == 0
    high_end = place == line - 1

    def span(k):
        return slice(k * lanes, (k + 1) * lanes)

    pairs = ((k_in, k_ref), (v_in, v_ref), (grad_in, grad_ref), (q_in, q_ref))
    copies = [pltpu.make_async_copy(a, b, loads.at[i]) for i, (a, b) in enumerate(pairs)]
    for copy in copies:
        copy.start()

    barrier = pltpu.get_barrier_semaphore()

    def greet(device):
        pl.semaphore_signal(barrier, inc=1, device_id=device, device_id_type=MESH)

    greet({"seq": other})
    for b in range(line_bits):
        greet({"seq": flip(me, 2 << b)})
    for r in range(1, heads):
        greet({"head": flip(head, r)})

    @pl.when(place < line - 1)
    def _():
        greet({"seq": above})

    @pl.when(place > 0)
    def _():
        greet({"seq": below})

    def remote(src, dst, send, recv, device):
        return pltpu.make_async_remote_copy(
            src_ref=src,
            dst_ref=dst,
            send_sem=send,
            recv_sem=recv,
            device_id=device,
            device_id_type=MESH,
        )

    def state_copy():
        return remote(
            state.at[pl.ds((1 - side) * half, half)],
            pair_state,
            state_send.at[0],
            state_recv.at[0],
            {"seq": other},
        )

    def line_copy(b):
        return remote(
            block.at[b],
            line_state.at[b],
            state_send.at[1 + b],
            state_recv.at[1 + b],
            {"seq": flip(me, 2 << b)},
        )

    def give_copy():
        return remote(
            give,
            mix.at[pl.ds(side * half, half)],
            state_send.at[1 + line_bits],
            state_recv.at[1 + line_bits],
            {"seq": other},
        )

    def grad_copy():
        return remote(
            quarter,
            theirs.at[pl.ds(head * share, share)],
            grad_send.at[0],
            grad_recv.at[0],
            {"seq": other},
        )

    def share_copy(r, bit):
        owned = theirs.at[pl.ds(flip(head, r) * share, share)]
        slot = r ^ (1 << bit)
        return remote(
            owned, owned, grad_send.at[slot], grad_recv.at[slot], {"head": flip(head, 1 << bit)}
        )

    def square_copy(r):
        return remote(
            squares,
            squares_in.at[r - 1],
            square_send.at[r - 1],
            square_recv.at[r - 1],
            {"head": flip(head, r)},
        )

    def root_copy():
        return remote(root, root_in, root_send.at[0], root_recv.at[0], {"seq": other})

    def pair_copy(k):
        return remote(raw.at[k], came.at[k], pair_send.at[k], pair_recv.at[k], {"seq": other})

    def up_copy(k, d):
        return remote(
            part.at[k, d], rising.at[k, d], up_send.at[k, d], up_recv.at[k, d], {"seq": above}
        )

    def down_copy(k, d):
        return remote(
            part.at[k, d], falling.at[k, d], down_send.at[k, d], down_recv.at[k, d], {"seq": below}
        )

    copies[0].wait()
    copies[1].wait()
    for h in range(chunks):
        state[h] = matmul(k_ref[:, span(h)], v_ref[:, span(h)], TN)
    peers = line_bits + heads + jnp.where(place > 0, 1, 0) + jnp.where(place < line - 1, 1, 0)
    pl.semaphore_wait(barrier, peers)
    state_copy().start()

    copies[2].wait()
    tile = max(rows, lanes)
    for j in range(grad_ref.shape[1] // tile):
        flat = grad_ref[:, j * tile : (j + 1) * tile].T
        for i in range(tile // rows):
            owner = j * (tile // rows) + i
            turned[owner % 2, owner // 2] = flat[i * rows : (i + 1) * rows]
    quarter[...] = turned[1 - side, pl.ds(head * share, share)].astype(jnp.float32)
    grad_copy().start()

    def near(h):
        weight = scale * level_ref[h, 0].astype(jnp.float32)
        scores = matmul(q_ref[:, span(h)], k_ref[:, span(h)], NT) * weight
        row = lax.broadcasted_iota(jnp.int32, scores.shape, 0)
        column = lax.broadcasted_iota(jnp.int32, scores.shape, 1)
        probs = jnp.where(column <= row, scores, 0.0).astype(jnp.bfloat16)
        raw[h] = matmul(probs, v_ref[:, span(h)])

    def level(i, number):
        return level_ref[side * half + i, number].astype(jnp.float32)

    copies[3].wait()
    own = pl.ds(side * half, half)
    state_copy().wait_recv()
    block[0] = state[own] + pair_state[...]
    done = 0
    for b in range(line_bits):
        upper = (place // (1 << b)) % 2
        last = b == line_bits - 1
        if last:

            @pl.when(upper == 0)
            def _():
                line_copy(b).start()
        else:
            line_copy(b).start()
        until = chunks * (b + 1) // line_bits
        for h in range(done, until):
            near(h)
        done = until
        if last:

            @pl.when(upper == 1)
            def _():
                line_copy(b).wait_recv()

            @pl.when(upper == 0)
            def _():
                line_state[b] = jnp.zeros(line_state.shape[1:], jnp.float32)
        else:
            line_copy(b).wait_recv()
            block[b + 1] = block[b] + line_state[b]
    for i in range(half):
        far = jnp.zeros((lanes, lanes), jnp.float32)
        for b in range(line_bits):
            upper = ((place // (1 << b)) % 2).astype(jnp.float32)
            far = far + (level(i, 2 + b) * upper) * line_state[b, i]
        first = level(i, 1)
        right = side.astype(jnp.float32)
        mix[side * half + i] = far + (first * right) * pair_state[i]
        give[i] = far + (first * (1.0 - right)) * state[side * half + i]
    give_copy().start()

    owned = [0]
    stages = list(reversed(range(head_bits)))
    grad_copy().wait_recv()

    def forward(bit):
        for r in owned:
            share_copy(r, bit).start()

    def collect(bit):
        for r in list(owned):
            share_copy(r, bit).wait_recv()
            owned.append(r ^ (1 << bit))

    forward(stages[0])
    give_copy().wait_recv()

    total = jnp.zeros((tokens, lanes), jnp.float32)
    for h in range(chunks):
        high, low = split(mix[h])
        query = q_ref[:, span(h)]
        value = raw[h] + scale * (matmul(query, high) + matmul(query, low))
        raw[h] = value
        pair_copy(h).start()
        total = total + value * value
    ones = jnp.ones((8, lanes), jnp.bfloat16)
    high, low = split(total)
    squares[...] = matmul(ones, high, NT) + matmul(ones, low, NT)
    for r in range(1, heads):
        square_copy(r).start()
    collect(stages[0])
    for r in range(1, heads):
        square_copy(r).wait_recv()
    whole = squares[...]
    for r in range(1, heads):
        whole = whole + squares_in[r - 1]
    root[...] = lax.rsqrt(whole / D + 1e-06)
    root_copy().start()
    for bit in stages[1:]:
        forward(bit)
        if bit != stages[-1]:
            collect(bit)
    inverse = root[...].T[:, :1]
    for h in range(chunks):
        normed_ref[:, span(h)] = (raw[h] * inverse).astype(jnp.bfloat16)
    root_copy().wait_recv()
    their_inverse = root_in[...].T[:, :1]
    if len(stages) > 1:
        collect(stages[-1])
    theirs_half[...] = theirs[...].reshape(theirs_half.shape).astype(jnp.bfloat16)

    def ends(k):
        @pl.when(low_end)
        def _():
            @pl.loop(0, line - 1)
            def _(i):
                up_copy(k, line - 1 - i).start()

        @pl.when(high_end)
        def _():
            @pl.loop(0, line - 1)
            def _(d):
                down_copy(k, d).start()

    def rise(k):
        @pl.loop(0, line - 1 - place)
        def _(i):
            d = line - 1 - i
            up_copy(k, d).wait_recv()
            part[k, d] = part[k, d] + rising[k, d]
            up_copy(k, d).start()

    def fall(k):
        @pl.loop(0, place)
        def _(d):
            down_copy(k, d).wait_recv()
            part[k, d] = part[k, d] + falling[k, d]
            down_copy(k, d).start()

    def middle(k):
        @pl.when(jnp.logical_and(place > 0, place < line // 2))
        def _():
            rise(k)
            fall(k)

        @pl.when(jnp.logical_and(place >= line // 2, place < line - 1))
        def _():
            fall(k)
            rise(k)

    for k in range(chunks):
        mine = turned[side].reshape(line * rows, tokens)
        product = matmul(mine, normed_ref[:, span(k)])
        pair_copy(k).wait_recv()
        there = (came[k] * their_inverse).astype(jnp.bfloat16)
        product = product + matmul(theirs_half[...], there)
        part[k] = product.reshape(part.shape[1:])
        ends(k)
        if k:
            middle(k - 1)
    middle(chunks - 1)

    for k in range(chunks):
        out_ref[:, span(k)] = part[k, place]

        @pl.when(place > 0)
        def _():
            up_copy(k, place).wait_recv()
            out_ref[:, span(k)] = out_ref[:, span(k)] + rising[k, place]

        @pl.when(place < line - 1)
        def _():
            down_copy(k, place).wait_recv()
            out_ref[:, span(k)] = out_ref[:, span(k)] + falling[k, place]

    state_copy().wait_send()
    for b in range(line_bits - 1):
        line_copy(b).wait_send()

    @pl.when((place // (line // 2)) % 2 == 0)
    def _():
        line_copy(line_bits - 1).wait_send()

    give_copy().wait_send()
    grad_copy().wait_send()
    held = [0]
    for bit in stages:
        for r in list(held):
            share_copy(r, bit).wait_send()
            held.append(r ^ (1 << bit))
    for r in range(1, heads):
        square_copy(r).wait_send()
    root_copy().wait_send()
    for k in range(chunks):
        pair_copy(k).wait_send()

        @pl.loop(place + 1, line)
        def _(d):
            up_copy(k, d).wait_send()

        @pl.loop(0, place)
        def _(d):
            down_copy(k, d).wait_send()


def body(queries, keys, values, level_weights, out_grad):
    tokens, width = queries.shape
    assert tokens == GROUP
    count = lax.axis_size("seq")
    heads = lax.axis_size("head")
    line = count // 2
    line_bits = line.bit_length() - 1
    lanes = D // HEADS
    chunks = width // lanes
    half = chunks // 2
    rows = out_grad.shape[1] // count
    slots = (chunks, line, rows, lanes)
    states = (half, lanes, lanes)
    vmem = pl.BlockSpec(memory_space=pltpu.VMEM)
    smem = pl.BlockSpec(memory_space=pltpu.SMEM)
    away = pl.BlockSpec(memory_space=pl.ANY)
    f32 = jnp.float32
    dma = pltpu.SemaphoreType.DMA
    return pl.pallas_call(
        functools.partial(kernel, line, heads),
        out_shape=(
            jax.ShapeDtypeStruct((tokens, width), jnp.bfloat16),
            jax.ShapeDtypeStruct((rows, width), f32),
        ),
        in_specs=[away, away, away, smem, away],
        out_specs=(vmem, vmem),
        scratch_shapes=[
            pltpu.VMEM(queries.shape, queries.dtype),
            pltpu.VMEM(keys.shape, keys.dtype),
            pltpu.VMEM(values.shape, values.dtype),
            pltpu.VMEM(out_grad.shape, out_grad.dtype),
            pltpu.SemaphoreType.DMA((4,)),
            pltpu.VMEM((chunks, lanes, lanes), f32),
            pltpu.VMEM(states, f32),
            pltpu.VMEM((line_bits, *states), f32),
            pltpu.VMEM((line_bits, *states), f32),
            pltpu.VMEM(states, f32),
            pltpu.VMEM((chunks, lanes, lanes), f32),
            pltpu.VMEM((2, line, rows, tokens), jnp.bfloat16),
            pltpu.VMEM((line // heads, rows, tokens), f32),
            pltpu.VMEM((line, rows, tokens), f32),
            pltpu.VMEM((line * rows, tokens), jnp.bfloat16),
            pltpu.VMEM((chunks, tokens, lanes), f32),
            pltpu.VMEM((chunks, tokens, lanes), f32),
            pltpu.VMEM((8, tokens), f32),
            pltpu.VMEM((heads - 1, 8, tokens), f32),
            pltpu.VMEM((8, tokens), f32),
            pltpu.VMEM((8, tokens), f32),
            pltpu.VMEM(slots, f32),
            pltpu.VMEM(slots, f32),
            pltpu.VMEM(slots, f32),
            dma((2 + line_bits,)),
            dma((2 + line_bits,)),
            dma((heads,)),
            dma((heads,)),
            dma((heads - 1,)),
            dma((heads - 1,)),
            dma((1,)),
            dma((1,)),
            dma((chunks,)),
            dma((chunks,)),
            dma((chunks, line)),
            dma((chunks, line)),
            dma((chunks, line)),
            dma((chunks, line)),
        ],
        compiler_params=pltpu.CompilerParams(
            collective_id=0, has_side_effects=True, vmem_limit_bytes=60 << 20
        ),
    )(queries, keys, values, level_weights, out_grad)


def solution(mesh):
    return jax.shard_map(
        body,
        mesh=mesh,
        in_specs=(
            P("seq", "head"),
            P("seq", "head"),
            P("seq", "head"),
            P("head", None),
            P("seq", None),
        ),
        out_specs=(P("seq", "head"), P("seq", "head")),
        check_vma=False,
    )
```

```python
import functools

import jax
import jax.numpy as jnp
from jax import lax
from jax.experimental import pallas as pl
from jax.experimental.pallas import tpu as pltpu
from jax.sharding import PartitionSpec as P

D = 2048
HEADS = 16
GROUP = 512
PIECES = 2
MESH = pl.DeviceIdType.MESH
NT = (((1,), (1,)), ((), ()))
TN = (((0,), (0,)), ((), ()))


def flip(index, mask):
    bit = 1
    while bit <= mask:
        if mask & bit:
            index = index + bit - 2 * bit * ((index // bit) % 2)
        bit *= 2
    return index


def matmul(a, b, dims=(((1,), (0,)), ((), ()))):
    return lax.dot_general(a, b, dims, preferred_element_type=jnp.float32)


def split(x):
    high = x.astype(jnp.bfloat16)
    return high, (x - high.astype(jnp.float32)).astype(jnp.bfloat16)


def kernel(
    line,
    heads,
    q_in,
    k_in,
    v_in,
    level_ref,
    grad_in,
    normed_ref,
    out_ref,
    q_ref,
    k_ref,
    v_ref,
    grad_ref,
    loads,
    state,
    pair_state,
    block,
    line_state,
    give,
    mix,
    turned,
    quarter,
    theirs,
    theirs_half,
    raw,
    came,
    squares,
    squares_in,
    root,
    root_in,
    part,
    rising,
    falling,
    state_send,
    state_recv,
    grad_send,
    grad_recv,
    square_send,
    square_recv,
    root_send,
    root_recv,
    pair_send,
    pair_recv,
    up_send,
    up_recv,
    down_send,
    down_recv,
):
    me = lax.axis_index("seq")
    head = lax.axis_index("head")
    place = me // 2
    side = me % 2
    other = flip(me, 1)
    above = me + 2
    below = me - 2
    tokens, width = q_ref.shape
    lanes = D // HEADS
    chunks = width // lanes
    half = chunks // 2
    rows = out_ref.shape[0]
    line_bits = line.bit_length() - 1
    head_bits = heads.bit_length() - 1
    share = line // heads
    piece = rows // PIECES
    stages = list(reversed(range(head_bits)))
    held = [[0]]
    for bit in stages:
        held.append(held[-1] + [r ^ (1 << bit) for r in held[-1]])
    scale = lanes ** (-0.5)
    low_end = place == 0
    high_end = place == line - 1

    def span(k):
        return slice(k * lanes, (k + 1) * lanes)

    pairs = ((k_in, k_ref), (v_in, v_ref), (grad_in, grad_ref), (q_in, q_ref))
    copies = [pltpu.make_async_copy(a, b, loads.at[i]) for i, (a, b) in enumerate(pairs)]
    for copy in copies:
        copy.start()

    barrier = pltpu.get_barrier_semaphore()

    def greet(device):
        pl.semaphore_signal(barrier, inc=1, device_id=device, device_id_type=MESH)

    greet({"seq": other})
    for b in range(line_bits):
        greet({"seq": flip(me, 2 << b)})
    for r in range(1, heads):
        greet({"head": flip(head, r)})

    @pl.when(place < line - 1)
    def _():
        greet({"seq": above})

    @pl.when(place > 0)
    def _():
        greet({"seq": below})

    def remote(src, dst, send, recv, device):
        return pltpu.make_async_remote_copy(
            src_ref=src,
            dst_ref=dst,
            send_sem=send,
            recv_sem=recv,
            device_id=device,
            device_id_type=MESH,
        )

    def state_copy():
        return remote(
            state.at[pl.ds((1 - side) * half, half)],
            pair_state,
            state_send.at[0],
            state_recv.at[0],
            {"seq": other},
        )

    def line_copy(b):
        return remote(
            block.at[b],
            line_state.at[b],
            state_send.at[1 + b],
            state_recv.at[1 + b],
            {"seq": flip(me, 2 << b)},
        )

    def give_copy():
        return remote(
            give,
            mix.at[pl.ds(side * half, half)],
            state_send.at[1 + line_bits],
            state_recv.at[1 + line_bits],
            {"seq": other},
        )

    def grad_copy(p):
        return remote(
            quarter.at[:, pl.ds(p * piece, piece)],
            theirs.at[pl.ds(head * share, share), pl.ds(p * piece, piece)],
            grad_send.at[0, p],
            grad_recv.at[0, p],
            {"seq": other},
        )

    def share_copy(r, bit, p):
        owned = theirs.at[pl.ds(flip(head, r) * share, share), pl.ds(p * piece, piece)]
        slot = r ^ (1 << bit)
        return remote(
            owned,
            owned,
            grad_send.at[slot, p],
            grad_recv.at[slot, p],
            {"head": flip(head, 1 << bit)},
        )

    def square_copy(r):
        return remote(
            squares,
            squares_in.at[r - 1],
            square_send.at[r - 1],
            square_recv.at[r - 1],
            {"head": flip(head, r)},
        )

    def root_copy():
        return remote(root, root_in, root_send.at[0], root_recv.at[0], {"seq": other})

    def pair_copy(k):
        return remote(raw.at[k], came.at[k], pair_send.at[k], pair_recv.at[k], {"seq": other})

    def up_copy(k, d):
        return remote(
            part.at[k, d], rising.at[k, d], up_send.at[k, d], up_recv.at[k, d], {"seq": above}
        )

    def down_copy(k, d):
        return remote(
            part.at[k, d], falling.at[k, d], down_send.at[k, d], down_recv.at[k, d], {"seq": below}
        )

    copies[0].wait()
    copies[1].wait()
    for h in range(chunks):
        state[h] = matmul(k_ref[:, span(h)], v_ref[:, span(h)], TN)
    peers = line_bits + heads + jnp.where(place > 0, 1, 0) + jnp.where(place < line - 1, 1, 0)
    pl.semaphore_wait(barrier, peers)
    state_copy().start()

    copies[2].wait()
    tile = max(rows, lanes)
    for j in range(grad_ref.shape[1] // tile):
        flat = grad_ref[:, j * tile : (j + 1) * tile].T
        for i in range(tile // rows):
            owner = j * (tile // rows) + i
            turned[owner % 2, owner // 2] = flat[i * rows : (i + 1) * rows]
    quarter[...] = turned[1 - side, pl.ds(head * share, share)].astype(jnp.float32)
    for p in range(PIECES):
        grad_copy(p).start()

    def forward(i, p):
        for r in held[i]:
            share_copy(r, stages[i], p).start()

    def collect(i, p):
        for r in held[i]:
            share_copy(r, stages[i], p).wait_recv()

    def near(h):
        weight = scale * level_ref[h, 0].astype(jnp.float32)
        scores = matmul(q_ref[:, span(h)], k_ref[:, span(h)], NT) * weight
        row = lax.broadcasted_iota(jnp.int32, scores.shape, 0)
        column = lax.broadcasted_iota(jnp.int32, scores.shape, 1)
        probs = jnp.where(column <= row, scores, 0.0).astype(jnp.bfloat16)
        raw[h] = matmul(probs, v_ref[:, span(h)])

    def level(i, number):
        return level_ref[side * half + i, number].astype(jnp.float32)

    copies[3].wait()
    own = pl.ds(side * half, half)
    state_copy().wait_recv()
    block[0] = state[own] + pair_state[...]
    done = 0
    for b in range(line_bits):
        upper = (place // (1 << b)) % 2
        last = b == line_bits - 1
        if last:

            @pl.when(upper == 0)
            def _():
                line_copy(b).start()
        else:
            line_copy(b).start()
        until = chunks * (b + 1) // line_bits
        for h in range(done, until):
            near(h)
        done = until
        if last:
            grad_copy(0).wait_recv()
            forward(0, 0)

            @pl.when(upper == 1)
            def _():
                line_copy(b).wait_recv()

            @pl.when(upper == 0)
            def _():
                line_state[b] = jnp.zeros(line_state.shape[1:], jnp.float32)
        else:
            line_copy(b).wait_recv()
            block[b + 1] = block[b] + line_state[b]
    for i in range(half):
        far = jnp.zeros((lanes, lanes), jnp.float32)
        for b in range(line_bits):
            upper = ((place // (1 << b)) % 2).astype(jnp.float32)
            far = far + (level(i, 2 + b) * upper) * line_state[b, i]
        first = level(i, 1)
        right = side.astype(jnp.float32)
        mix[side * half + i] = far + (first * right) * pair_state[i]
        give[i] = far + (first * (1.0 - right)) * state[side * half + i]
    give_copy().start()

    for p in range(1, PIECES):
        grad_copy(p).wait_recv()
        forward(0, p)
    give_copy().wait_recv()

    total = jnp.zeros((tokens, lanes), jnp.float32)
    for h in range(chunks):
        high, low = split(mix[h])
        query = q_ref[:, span(h)]
        value = raw[h] + scale * (matmul(query, high) + matmul(query, low))
        raw[h] = value
        pair_copy(h).start()
        total = total + value * value
    ones = jnp.ones((8, lanes), jnp.bfloat16)
    high, low = split(total)
    squares[...] = matmul(ones, high, NT) + matmul(ones, low, NT)
    for r in range(1, heads):
        square_copy(r).start()
    collect(0, 0)
    forward(1, 0)
    for r in range(1, heads):
        square_copy(r).wait_recv()
    whole = squares[...]
    for r in range(1, heads):
        whole = whole + squares_in[r - 1]
    root[...] = lax.rsqrt(whole / D + 1e-06)
    root_copy().start()
    for p in range(1, PIECES):
        collect(0, p)
        forward(1, p)
    inverse = root[...].T[:, :1]
    for h in range(chunks):
        normed_ref[:, span(h)] = (raw[h] * inverse).astype(jnp.bfloat16)
    root_copy().wait_recv()
    their_inverse = root_in[...].T[:, :1]
    for i in range(1, head_bits):
        for p in range(PIECES):
            if i > 1:
                forward(i, p)
            collect(i, p)
    theirs_half[...] = theirs[...].reshape(theirs_half.shape).astype(jnp.bfloat16)

    def ends(k):
        @pl.when(low_end)
        def _():
            @pl.loop(0, line - 1)
            def _(i):
                up_copy(k, line - 1 - i).start()

        @pl.when(high_end)
        def _():
            @pl.loop(0, line - 1)
            def _(d):
                down_copy(k, d).start()

    def rise(k):
        @pl.loop(0, line - 1 - place)
        def _(i):
            d = line - 1 - i
            up_copy(k, d).wait_recv()
            part[k, d] = part[k, d] + rising[k, d]
            up_copy(k, d).start()

    def fall(k):
        @pl.loop(0, place)
        def _(d):
            down_copy(k, d).wait_recv()
            part[k, d] = part[k, d] + falling[k, d]
            down_copy(k, d).start()

    def middle(k):
        @pl.when(jnp.logical_and(place > 0, place < line // 2))
        def _():
            rise(k)
            fall(k)

        @pl.when(jnp.logical_and(place >= line // 2, place < line - 1))
        def _():
            fall(k)
            rise(k)

    for k in range(chunks):
        mine = turned[side].reshape(line * rows, tokens)
        product = matmul(mine, normed_ref[:, span(k)])
        pair_copy(k).wait_recv()
        there = (came[k] * their_inverse).astype(jnp.bfloat16)
        product = product + matmul(theirs_half[...], there)
        part[k] = product.reshape(part.shape[1:])
        ends(k)
        if k:
            middle(k - 1)
    middle(chunks - 1)

    for k in range(chunks):
        out_ref[:, span(k)] = part[k, place]

        @pl.when(place > 0)
        def _():
            up_copy(k, place).wait_recv()
            out_ref[:, span(k)] = out_ref[:, span(k)] + rising[k, place]

        @pl.when(place < line - 1)
        def _():
            down_copy(k, place).wait_recv()
            out_ref[:, span(k)] = out_ref[:, span(k)] + falling[k, place]

    state_copy().wait_send()
    for b in range(line_bits - 1):
        line_copy(b).wait_send()

    @pl.when((place // (line // 2)) % 2 == 0)
    def _():
        line_copy(line_bits - 1).wait_send()

    give_copy().wait_send()
    for p in range(PIECES):
        grad_copy(p).wait_send()
        for i in range(head_bits):
            for r in held[i]:
                share_copy(r, stages[i], p).wait_send()
    for r in range(1, heads):
        square_copy(r).wait_send()
    root_copy().wait_send()
    for k in range(chunks):
        pair_copy(k).wait_send()

        @pl.loop(place + 1, line)
        def _(d):
            up_copy(k, d).wait_send()

        @pl.loop(0, place)
        def _(d):
            down_copy(k, d).wait_send()


def body(queries, keys, values, level_weights, out_grad):
    tokens, width = queries.shape
    assert tokens == GROUP
    count = lax.axis_size("seq")
    heads = lax.axis_size("head")
    line = count // 2
    line_bits = line.bit_length() - 1
    lanes = D // HEADS
    chunks = width // lanes
    half = chunks // 2
    rows = out_grad.shape[1] // count
    slots = (chunks, line, rows, lanes)
    states = (half, lanes, lanes)
    vmem = pl.BlockSpec(memory_space=pltpu.VMEM)
    smem = pl.BlockSpec(memory_space=pltpu.SMEM)
    away = pl.BlockSpec(memory_space=pltpu.MemorySpace.HBM)
    f32 = jnp.float32
    dma = pltpu.SemaphoreType.DMA
    return pl.pallas_call(
        functools.partial(kernel, line, heads),
        out_shape=(
            jax.ShapeDtypeStruct((tokens, width), jnp.bfloat16),
            jax.ShapeDtypeStruct((rows, width), f32),
        ),
        in_specs=[away, away, away, smem, away],
        out_specs=(vmem, vmem),
        scratch_shapes=[
            pltpu.VMEM(queries.shape, queries.dtype),
            pltpu.VMEM(keys.shape, keys.dtype),
            pltpu.VMEM(values.shape, values.dtype),
            pltpu.VMEM(out_grad.shape, out_grad.dtype),
            pltpu.SemaphoreType.DMA((4,)),
            pltpu.VMEM((chunks, lanes, lanes), f32),
            pltpu.VMEM(states, f32),
            pltpu.VMEM((line_bits, *states), f32),
            pltpu.VMEM((line_bits, *states), f32),
            pltpu.VMEM(states, f32),
            pltpu.VMEM((chunks, lanes, lanes), f32),
            pltpu.VMEM((2, line, rows, tokens), jnp.bfloat16),
            pltpu.VMEM((line // heads, rows, tokens), f32),
            pltpu.VMEM((line, rows, tokens), f32),
            pltpu.VMEM((line * rows, tokens), jnp.bfloat16),
            pltpu.VMEM((chunks, tokens, lanes), f32),
            pltpu.VMEM((chunks, tokens, lanes), f32),
            pltpu.VMEM((8, tokens), f32),
            pltpu.VMEM((heads - 1, 8, tokens), f32),
            pltpu.VMEM((8, tokens), f32),
            pltpu.VMEM((8, tokens), f32),
            pltpu.VMEM(slots, f32),
            pltpu.VMEM(slots, f32),
            pltpu.VMEM(slots, f32),
            dma((2 + line_bits,)),
            dma((2 + line_bits,)),
            dma((heads, PIECES)),
            dma((heads, PIECES)),
            dma((heads - 1,)),
            dma((heads - 1,)),
            dma((1,)),
            dma((1,)),
            dma((chunks,)),
            dma((chunks,)),
            dma((chunks, line)),
            dma((chunks, line)),
            dma((chunks, line)),
            dma((chunks, line)),
        ],
        compiler_params=pltpu.CompilerParams(
            collective_id=0, has_side_effects=True, vmem_limit_bytes=60 << 20
        ),
    )(queries, keys, values, level_weights, out_grad)


def solution(mesh):
    return jax.shard_map(
        body,
        mesh=mesh,
        in_specs=(
            P("seq", "head"),
            P("seq", "head"),
            P("seq", "head"),
            P("head", None),
            P("seq", None),
        ),
        out_specs=(P("seq", "head"), P("seq", "head")),
        check_vma=False,
    )
```
